32 devices in a mesh: grp: 2 (over x), seq: 8 (over z, y), tile: 2 (over core).
Axes of the slice: x: 2, y: 2, z: 4, core: 2. Of those that a mesh axis runs over, the one named last changes fastest.
Arguments:
- tiles: bfloat16 [16384, 1536], P(('grp', 'seq', 'tile')), parts along dimension 0, may hold values from -6 to 6
- producer: int32 [8192, 1], P('grp'), parts along dimension 0, may hold values from 0 to 15; in each aligned block of 256 rows (0 to 255, 256 to 511, ...) at most 32 rows name the same one
- slide_lengths: int32 [8], P('grp'), parts along dimension 0, may hold values from 1 to 2048, 4096 in all
- dilation: int32 [4], replicated, may hold values from 1 to 8, as said below
- in_weight: bfloat16 [1536, 768], replicated, may hold values from -0.15625 to 0.15625
- in_bias: float32 [768], replicated, may hold values from -3 to 3
- norm_gain: float32 [768], replicated, may hold values from 0.1 to 1.9
- norm_bias: float32 [768], replicated, may hold values from -3 to 3
- qkv_weight: bfloat16 [3, 768, 768], P(None, None, 'tile'), may hold values from -1.5 to 1.5
- qkv_bias: float32 [3, 768], P(None, 'tile'), may hold values from -3 to 3
- out_weight: bfloat16 [768, 768], P('tile'), may hold values from -0.21875 to 0.21875
- out_bias: float32 [768], replicated, may hold values from -3 to 3
Outputs:
- embedded: bfloat16 [8192, 768], P(('grp', 'seq', 'tile')), parts along dimension 0
- branch: bfloat16 [8192, 768], P(('grp', 'seq', 'tile')), parts along dimension 0
The draws below stay inside these ranges and needn't reach their ends.
There are 2 independent parts, one for each index of `grp`. The reference program is written for one: setup_inputs(seed, part) draws one part's arguments, and reference() takes and returns one part's arrays. A program takes and returns all parts, laid end to end along the dimension named above; an argument that names none is the same for every part. Nothing has to cross between parts.
Inputs may be any that keep to these rules, and one draw needn't show every extreme that they name: In each aligned block of 256 positions no producer appears more than 32 times; in every draw some producer appears exactly 32 times in some block, and every producer appears somewhere. `slide_lengths`: the lengths sum to 4096; the largest is exactly 2048. Every entry is a power of two; in every draw some group has dilation 1 and some group has 8.
All inputs are finite; a program needn't handle non-finite values.
Results may differ from the reference program's by a relative error of at most 0.011.
Values may be sent and summed in bfloat16 or wider, within the bound.
A program may use at most 64 MiB of HBM per device.

```python
import math
import jax
import jax.numpy as jnp
import numpy as np
from jax import lax

D = 768
HEADS = 16
IN_DIM = 1536
GROUPS = 4
SPARSE = 512
WINDOW = 4096
PRODUCERS = 16
MOST = 32
DMAX = 8
SLIDES = 4
SLIDE_MOST = 2048
N_SEQ = 8
N_TILE = 2


def draw_dilation(key, part):
    levels = int(DMAX).bit_length() - 1
    expos = jax.random.randint(jax.random.fold_in(key, 11), (GROUPS,), 0, levels + 1)
    order = jax.random.permutation(jax.random.fold_in(key, 12), GROUPS)
    expos = jnp.where(order == 0, 0, expos)
    expos = jnp.where(order == 1, levels, expos)
    return jnp.left_shift(jnp.ones((GROUPS,), jnp.int32), expos.astype(jnp.int32))


def draw_qkv_weight(key, part):
    base = jax.random.normal(jax.random.fold_in(key, 21), (3, D, D), jnp.float32) / jnp.sqrt(jnp.float32(D))
    return jnp.clip(base, -1.5, 1.5).astype(jnp.bfloat16)


def block_scale(stream_key, dims, split, least, top_value):
    level, own = 1.0, jax.random.fold_in(stream_key, 6)
    for axis_at, blocks in split:
        draws = jnp.exp(jax.random.uniform(jax.random.fold_in(own, axis_at), (blocks,), jnp.float32, least / len(split), top_value / len(split)))
        level = level * jnp.repeat(draws, dims[axis_at] // blocks).reshape([-1 if axis == axis_at else 1 for axis in range(len(dims))])
    return level


def length_profile(count, total, reach, skew):
    portions = [(1 << 20) // math.isqrt(grade ** skew) + 1 for grade in range(2, count + 1)]
    surplus, holding = total - reach - (count - 1), [1] * (count - 1)
    while surplus > 0:
        movable = [i for i in range(count - 1) if holding[i] < reach]
        mass, left = sum([portions[i] for i in movable]), surplus
        for i in movable:
            addition = min(reach - holding[i], max(1, left * portions[i] // mass), surplus)
            holding[i] = holding[i] + addition
            surplus = surplus - addition
    return np.array([reach] + holding)


def ragged_sizes(rng, number_of, total, limit, skew):
    if number_of == 2:
        one = jax.random.randint(rng, (), max(1, total - limit), min(limit, total - 1) + 1)
        return jnp.stack([one, total - one])
    sizes = jnp.asarray(length_profile(number_of, total, limit, skew), jnp.int32)
    pairs = (number_of - 1) // 2
    source_of, taker = sizes[1:1 + 2 * pairs:2], sizes[2:2 + 2 * pairs:2]
    room = jnp.minimum(source_of - 1, limit - taker)
    passed = jax.random.randint(jax.random.fold_in(rng, 1), (pairs,), 0, 1 << 20) % (room + 1)
    sizes = sizes.at[1:1 + 2 * pairs:2].set(source_of - passed).at[2:2 + 2 * pairs:2].set(taker + passed)
    return sizes[jax.random.permutation(jax.random.fold_in(rng, 2), number_of)]


def assign_block(stream_key, own, number, rows, amount, top, bound, lean):
    order = jax.random.permutation(stream_key, amount)
    packed, ordinary = shares(amount, rows * top, bound, lean, True), shares(amount, rows * top, bound, lean, False)
    places = jnp.arange(amount)

    def named(sizes, offset_by):
        used = int((sizes > 0).sum())
        fixed = max(1, used // 4)
        passed = fixed + (places - fixed + offset_by * (used - fixed)) % max(1, amount - fixed)
        return jnp.zeros((amount,), jnp.int32).at[order[jnp.where(places < fixed, places, passed)]].set(jnp.asarray(sizes, jnp.int32))

    sizes = jnp.where(number % 4 == 0, named(packed, number // 4), named(ordinary, number - number // 4 - 1))
    mixed = jax.random.permutation(jax.random.fold_in(own, 3), amount)
    donor, receiver = mixed[0:amount // 2 * 2:2], mixed[1:amount // 2 * 2:2]
    room = jnp.minimum(sizes[donor] - 1, bound - sizes[receiver]) // 2
    room = jnp.where((donor == order[0]) | (receiver == order[0]) | (sizes[receiver] == 0), 0, jnp.maximum(room, 0))
    passed = jax.random.randint(jax.random.fold_in(own, 4), (amount // 2,), 0, 1 << 20) % (room + 1)
    sizes = sizes.at[donor].add(-passed).at[receiver].add(passed)
    items = jnp.searchsorted(jnp.cumsum(sizes), jnp.arange(rows * top), side="right").astype(jnp.int32)
    listing = items.reshape(top, rows).T
    listing = listing[jax.random.permutation(jax.random.fold_in(own, 1), rows)]
    offset_by = jax.random.randint(jax.random.fold_in(own, 2), (rows, 1), 0, top)
    return jnp.take_along_axis(listing, (jnp.arange(top)[None, :] + offset_by) % top, axis=1)


def shares(count, total, bound, slope, full):
    weights = [(1 << 20) // math.isqrt(grade ** slope) + 1 for grade in range(1, count + 1)]
    largest = bound if full else min(bound, max(-(-total // count), total * weights[0] // sum(weights)))
    least = 1 if total - largest >= count - 1 else 0
    holding, spare = [largest] + [least] * (count - 1), total - largest - least * (count - 1)
    while spare > 0:
        free = [i for i in range(1, count) if holding[i] < largest] or [i for i in range(1, count) if holding[i] < bound]
        mass, left = sum([weights[i] for i in free]), spare
        for i in free:
            extra = min(bound - holding[i], max(1, left * weights[i] // mass), spare)
            holding[i] = holding[i] + extra
            spare = spare - extra
    return np.array(holding)


def noise(own_key, extent, width, limit, split=(), kind=jnp.bfloat16):
    loudness = block_scale(own_key, extent, split, -0.22, 0.18) if split else 1.0
    array = jax.random.normal(own_key, extent, jnp.float32) * width * loudness
    return jnp.minimum(jnp.maximum(array, -limit), limit).astype(kind)


def setup_inputs(seed: int = 0, part: int = 0) -> dict:
    streams_of = jax.random.split(jax.random.key(seed), 13)
    own_keys = jax.random.split(jax.random.fold_in(streams_of[12], part), 13)
    tiles = noise(own_keys[0], (PRODUCERS * SPARSE, IN_DIM), 1.0, 6.0, ((0, 16),))
    producer_keys = jax.random.split(jax.random.fold_in(own_keys[1], 1), WINDOW // (SPARSE // 2))
    producer_turns = jax.random.permutation(jax.random.fold_in(own_keys[1], 3), WINDOW // (SPARSE // 2))
    producer = jax.vmap(lambda own, number: assign_block(jax.random.fold_in(own_keys[1], 2), own, number, SPARSE // 2, PRODUCERS, 1, MOST, 2))(producer_keys, producer_turns).reshape((WINDOW, 1))
    slide_lengths = ragged_sizes(own_keys[2], SLIDES, WINDOW, SLIDE_MOST, 1).astype(jnp.int32)
    dilation = draw_dilation(jax.random.fold_in(streams_of[12], 71), part)
    in_weight = noise(streams_of[4], (IN_DIM, D), IN_DIM ** -0.5, 0.15625)
    in_bias = noise(streams_of[5], (D,), 0.5, 3.0, (), jnp.float32)
    norm_gain = jnp.clip(1.0 + 0.18 * jax.random.normal(streams_of[6], (D,), jnp.float32), 0.1, 1.9)
    norm_bias = noise(streams_of[7], (D,), 0.5, 3.0, (), jnp.float32)
    qkv_weight = draw_qkv_weight(jax.random.fold_in(streams_of[12], 71), part)
    qkv_bias = noise(streams_of[9], (3, D), 0.5, 3.0, ((1, 2),), jnp.float32)
    out_weight = noise(streams_of[10], (D, D), D ** -0.5, 0.21875, ((0, 2),))
    out_bias = noise(streams_of[11], (D,), 0.5, 3.0, (), jnp.float32)
    return {"tiles": tiles, "producer": producer, "slide_lengths": slide_lengths, "dilation": dilation, "in_weight": in_weight, "in_bias": in_bias, "norm_gain": norm_gain, "norm_bias": norm_bias, "qkv_weight": qkv_weight, "qkv_bias": qkv_bias, "out_weight": out_weight, "out_bias": out_bias}


def segment_attention(queries, key_rows, values, slide_ids, score_scale):
    scores = jnp.einsum('qhd,khd->hqk', queries.astype(jnp.float32), key_rows.astype(jnp.float32)) * score_scale
    allowed = slide_ids[:, None] == slide_ids[None, :]
    scores = jnp.where(allowed[None], scores, -1e+30)
    row_peak = lax.optimization_barrier(jnp.max(scores, axis=2, keepdims=True))
    exponent = jnp.where(allowed[None], jnp.exp(scores - row_peak), 0.0)
    weights = (exponent / lax.optimization_barrier(jnp.sum(exponent, axis=2, keepdims=True))).astype(jnp.bfloat16)
    mixed_rows = jnp.einsum('hqk,khd->qhd', weights.astype(jnp.float32), values.astype(jnp.float32))
    return mixed_rows.astype(jnp.bfloat16)

def reference(tiles, producer, slide_lengths, dilation, in_weight, in_bias, norm_gain, norm_bias, qkv_weight, qkv_bias, out_weight, out_bias):
    devices = N_SEQ * N_TILE
    owners = producer[:, 0]
    onehot = (owners[:, None] == jnp.arange(devices, dtype=jnp.int32)[None, :]).astype(jnp.int32)
    arrival_rank = lax.optimization_barrier(jnp.sum((jnp.cumsum(onehot, axis=0) - 1) * onehot, axis=1))
    raw_rows = jnp.take(tiles, (owners * SPARSE + arrival_rank).astype(jnp.int32), axis=0)
    embedded = (jnp.dot(raw_rows, in_weight, preferred_element_type=jnp.float32) + in_bias).astype(jnp.bfloat16)
    widened = embedded.astype(jnp.float32)
    center = widened - lax.optimization_barrier(jnp.mean(widened, axis=1, keepdims=True))
    spread = lax.optimization_barrier(jnp.mean(center * center, axis=1, keepdims=True))
    normed = (center * lax.rsqrt(spread + 1e-05) * norm_gain + norm_bias).astype(jnp.bfloat16)
    triple = [(jnp.dot(normed, qkv_weight[member_id], preferred_element_type=jnp.float32) + qkv_bias[member_id]).astype(jnp.bfloat16) for member_id in range(3)]
    head_dim = D // HEADS
    per_group = HEADS // GROUPS
    group_cols = per_group * head_dim
    score_scale = 1.0 / math.sqrt(head_dim)
    slide_ends = jnp.cumsum(slide_lengths)
    classes = WINDOW // SPARSE
    class_ids = jnp.arange(classes, dtype=jnp.int32)
    member_ids = jnp.arange(SPARSE, dtype=jnp.int32)
    outputs = []
    for group_id in range(GROUPS):
        rate = dilation[group_id]
        segment_ids = class_ids // rate
        residue = class_ids % rate
        positions = (segment_ids[:, None] * rate * SPARSE + member_ids[None, :] * rate + residue[:, None]).astype(jnp.int32)
        first = group_id * group_cols
        query_cols = triple[0][:, first:first + group_cols]
        key_cols = triple[1][:, first:first + group_cols]
        value_cols = triple[2][:, first:first + group_cols]

        def attend_class(index_row):
            queries = jnp.take(query_cols, index_row, axis=0).reshape(SPARSE, per_group, head_dim)
            key_rows = jnp.take(key_cols, index_row, axis=0).reshape(SPARSE, per_group, head_dim)
            values = jnp.take(value_cols, index_row, axis=0).reshape(SPARSE, per_group, head_dim)
            slide_ids = lax.optimization_barrier(jnp.sum((index_row[:, None] >= slide_ends[None, :]).astype(jnp.int32), axis=1))
            return segment_attention(queries, key_rows, values, slide_ids, score_scale).reshape(SPARSE, group_cols)
        results = lax.map(attend_class, positions)
        placed = jnp.zeros((WINDOW, group_cols), jnp.bfloat16).at[positions.reshape(-1)].set(results.reshape(-1, group_cols))
        outputs.append(placed)
    attended = jnp.concatenate(outputs, axis=1)
    branch = (jnp.dot(attended, out_weight, preferred_element_type=jnp.float32) + out_bias).astype(jnp.bfloat16)
    return (embedded, branch)
```

```python
import functools
import math

import jax
import jax.numpy as jnp
from jax import lax
from jax.experimental import pallas as pl
from jax.experimental.pallas import tpu as pltpu
from jax.sharding import PartitionSpec as P

HEADS = 16
MESH = pl.DeviceIdType.MESH
BF = jnp.bfloat16
F32 = jnp.float32
VMEM_CAP = 56 * 1024 * 1024


def bit_of(value, bit):
    return (value // (1 << bit)) % 2


def reversed_bits(value, bits):
    total = 0
    for bit in range(bits):
        total = total + bit_of(value, bit) * (1 << (bits - 1 - bit))
    return total


def partner(seq, bit, low):
    span = 1 << bit
    return (seq // (2 * span)) * (2 * span) + (1 - bit_of(seq, bit)) * span + low


def exact_dot(a, b):
    return jnp.dot(a, b, preferred_element_type=F32)


def exchange_plan(levels):
    return [(bit, turn) for bit in reversed(range(levels)) for turn in range(1 << bit)]


def hand_over(
    levels, tiles, weight, bias, pick, own, gain, shift, placed, rows, outbox, inbox,
    send_a, recv_a, send_b, recv_b, send_c, recv_c,
):
    seq_n, tile_n = lax.axis_size("seq"), lax.axis_size("tile")
    devices = seq_n * tile_n
    seq, core = lax.axis_index("seq"), lax.axis_index("tile")
    other = 1 - core
    me = seq * tile_n + core
    per_pair = outbox.shape[1]
    block = own.shape[0]
    width = outbox.shape[2]
    barrier = pltpu.get_barrier_semaphore()
    for k in range(1, devices):
        peer = (me + k) % devices
        pl.semaphore_signal(
            barrier, inc=1, device_id={"seq": peer // tile_n, "tile": peer % tile_n}, device_id_type=MESH
        )
    source = (exact_dot(tiles[...], weight[...]) + bias[...]).astype(BF)
    slots = devices * per_pair
    chosen = (pick[...] == lax.broadcasted_iota(jnp.int32, (slots, tiles.shape[0]), 1)).astype(BF)
    outbox[...] = exact_dot(chosen, source).reshape(devices, per_pair, width).astype(BF)
    pl.semaphore_wait(barrier, devices - 1)

    order = sorted(range(1, devices), key=lambda k: abs(k - devices // 2))
    first = []
    for k in order:
        peer = (me + k) % devices
        copy = pltpu.make_async_remote_copy(
            src_ref=outbox.at[peer], dst_ref=inbox.at[me], send_sem=send_a.at[k - 1], recv_sem=recv_a.at[k - 1],
            device_id={"seq": peer // tile_n, "tile": peer % tile_n}, device_id_type=MESH,
        )
        copy.start()
        first.append(copy)
    inbox[me] = outbox[me]
    onehot = (own[...] == lax.broadcasted_iota(jnp.int32, (block, 128), 1)).astype(F32)
    row_i = lax.broadcasted_iota(jnp.int32, (block, block), 0)
    col_i = lax.broadcasted_iota(jnp.int32, (block, block), 1)
    before = exact_dot((col_i < row_i).astype(BF), onehot.astype(BF))
    rank = jnp.sum(before * onehot, axis=1, keepdims=True).astype(jnp.int32)
    slot = own[...] * per_pair + rank
    landing = (slot == lax.broadcasted_iota(jnp.int32, (block, slots), 1)).astype(BF)
    span = 1 << levels
    stretch = block // span
    reorder = (reversed_bits(row_i // stretch, levels) + span * (row_i % stretch) == col_i).astype(BF)
    for copy in first:
        copy.wait_recv()
    got = inbox[...].astype(F32).reshape(slots, width).astype(BF)
    embedded = exact_dot(landing, got)
    placed[...] = embedded.astype(BF)
    center = embedded - jnp.mean(embedded, axis=1, keepdims=True)
    spread = jnp.mean(center * center, axis=1, keepdims=True)
    normed = (center * lax.rsqrt(spread + 1e-05) * gain[...] + shift[...]).astype(BF)
    rows[core, 0:block] = exact_dot(reorder, normed).astype(BF)

    second, forwards = [], []
    half = block // 2
    for at, (bit, turn) in enumerate(exchange_plan(levels)):
        count = block >> (bit + 1)
        to = partner(seq, bit, (seq + turn) % (1 << bit))
        start = pl.multiple_of(reversed_bits(to, bit + 1) * count, count)
        land = pl.multiple_of(block + half * bit + (seq % (1 << bit)) * count, count)
        copy = pltpu.make_async_remote_copy(
            src_ref=rows.at[core, pl.ds(start, count)], dst_ref=rows.at[core, pl.ds(land, count)],
            send_sem=send_b.at[at], recv_sem=recv_b.at[at],
            device_id={"seq": to, "tile": core}, device_id_type=MESH,
        )
        copy.start()
        second.append(copy)
    last = len(second)
    copy = pltpu.make_async_remote_copy(
        src_ref=rows.at[core, pl.ds(0, block)], dst_ref=rows.at[core, pl.ds(0, block)],
        send_sem=send_c.at[last], recv_sem=recv_c.at[last],
        device_id={"seq": seq, "tile": other}, device_id_type=MESH,
    )
    copy.start()
    forwards.append(copy)
    for at, (bit, turn) in reversed(list(enumerate(exchange_plan(levels)))):
        count = block >> (bit + 1)
        low = (seq % (1 << bit) + (1 << bit) - turn) % (1 << bit)
        land = pl.multiple_of(block + half * bit + low * count, count)
        second[at].wait_recv()
        copy = pltpu.make_async_remote_copy(
            src_ref=rows.at[core, pl.ds(land, count)], dst_ref=rows.at[core, pl.ds(land, count)],
            send_sem=send_c.at[at], recv_sem=recv_c.at[at],
            device_id={"seq": seq, "tile": other}, device_id_type=MESH,
        )
        copy.start()
        forwards.append(copy)
    for copy in first + second:
        copy.wait_send()
    for copy in forwards:
        copy.wait()


def chunk_list(seq, level, block):
    width = block >> level
    sub = reversed_bits(seq, level) * width
    found = [(sub, seq % (1 << level))]
    for bit in range(level):
        count = block >> (bit + 1)
        inner = sub - reversed_bits(seq, bit + 1) * count
        for low in range(1 << bit):
            found.append(
                (block + (block // 2) * bit + low * count + inner, partner(seq, bit, low) % (1 << level))
            )
    return [(pl.multiple_of(a, width), pl.multiple_of(c * width, width)) for a, c in found]


def attend(levels, slides, dil, ends, rows, weight, bias, back, picked, id_col, id_row, mixed):
    seq = lax.axis_index("seq")
    block = picked.shape[0] // 2
    total = 2 * block
    groups = dil.shape[0]
    group_cols = weight.shape[2] // groups
    head_dim = weight.shape[1] // HEADS
    heads_here = group_cols // head_dim
    factor = math.log2(math.e) / math.sqrt(head_dim)
    span = 1 << levels
    stretch = block // span
    back[...] = jnp.zeros_like(back)

    def slide_of(n, level):
        size = block >> level
        v = n % size
        pos = (
            ((seq >> level) << level) * total + ((n % block) // size) * total + (n // block) * block
            + seq % (1 << level)
            + (reversed_bits(v // stretch, levels - level) << level)
            + span * (v % stretch)
        )
        out = jnp.zeros_like(n)
        for at in range(slides):
            out = out + (pos >= ends[at]).astype(jnp.int32)
        return out

    for g in range(groups):
        offset = g * group_cols // 128 * 128
        wide = -(-(g * group_cols + group_cols - offset) // 128) * 128
        for level in range(levels + 1):
            @pl.when(dil[g] == 1 << level)
            def _():
                size = block >> level
                for side in range(2):
                    for start, put in chunk_list(seq, level, block):
                        picked[pl.ds(side * block + put, size), :] = rows[side, pl.ds(start, size), :]
                id_col[...] = slide_of(lax.broadcasted_iota(jnp.int32, (total, 1), 0), level)
                id_row[...] = slide_of(lax.broadcasted_iota(jnp.int32, (1, total), 1), level)

        x = picked[...]
        triple = [
            (exact_dot(x, weight[m, :, offset : offset + wide]) + bias[m : m + 1, offset : offset + wide]).astype(BF)
            for m in range(3)
        ]
        queries, keys, values = triple
        closed = jnp.where(id_col[...] == id_row[...], 0.0, -1e30)
        lane = lax.broadcasted_iota(jnp.int32, (1, wide), 1)
        result = jnp.zeros((total, wide), F32)
        for h in range(heads_here):
            low = g * group_cols - offset + h * head_dim
            inside = (lane >= low) & (lane < low + head_dim)
            scores = lax.dot_general(
                jnp.where(inside, queries, jnp.zeros((), BF)), keys, (((1,), (1,)), ((), ())),
                preferred_element_type=F32,
            ) + closed
            peak = jnp.max(scores, axis=1, keepdims=True)
            weights = jnp.exp2((scores - peak) * factor)
            norm = jnp.sum(weights, axis=1, keepdims=True)
            result = jnp.where(inside, exact_dot(weights.astype(BF), values) / norm, result)
        mixed[...] = result.astype(BF)
        for level in range(levels + 1):
            @pl.when(dil[g] == 1 << level)
            def _():
                size = block >> level
                for side in range(2):
                    for start, put in chunk_list(seq, level, block):
                        back[side, pl.ds(start, size), offset : offset + wide] += mixed[
                            pl.ds(side * block + put, size), :
                        ]


def give_back(
    levels, local_groups, dil, back, weight, bias, out, arrived, weights, send_a, recv_a, send_b, recv_b
):
    seq, core = lax.axis_index("seq"), lax.axis_index("tile")
    other = 1 - core
    block = out.shape[0]
    half = block // 2
    plan = exchange_plan(levels)
    barrier = pltpu.get_barrier_semaphore()
    peers = []
    for bit, turn in plan:
        to = partner(seq, bit, (seq + turn) % (1 << bit))
        peers += [{"seq": to, "tile": core}, {"seq": to, "tile": other}]
    sibling = {"seq": seq, "tile": other}
    for device in peers + [sibling]:
        pl.semaphore_signal(barrier, inc=1, device_id=device, device_id_type=MESH)
    pl.semaphore_wait(barrier, len(peers) + 1)
    copies = []
    for at, (bit, turn) in enumerate(plan):
        count = block >> (bit + 1)
        low = (seq + turn) % (1 << bit)
        start = pl.multiple_of(block + half * bit + low * count, count)
        land = pl.multiple_of(block + half * bit + (seq % (1 << bit)) * count, count)
        for rel in range(2):
            side = (core + rel) % 2
            copy = pltpu.make_async_remote_copy(
                src_ref=back.at[side, pl.ds(start, count)], dst_ref=arrived.at[core, pl.ds(land, count)],
                send_sem=send_a.at[2 * at + rel], recv_sem=recv_a.at[2 * at + rel],
                device_id={"seq": partner(seq, bit, low), "tile": side}, device_id_type=MESH,
            )
            copy.start()
            copies.append(copy)
    for at, (src, dst) in enumerate(
        [(back.at[other, pl.ds(0, block)], arrived.at[core, pl.ds(0, block)]), (weight, weights.at[core])]
    ):
        copy = pltpu.make_async_remote_copy(
            src_ref=src, dst_ref=dst, send_sem=send_b.at[at], recv_sem=recv_b.at[at],
            device_id=sibling, device_id_type=MESH,
        )
        copy.start()
        copies.append(copy)
    arrived[core, 0:block] = back[core, 0:block]
    weights[core] = weight[...]
    group_cols = weight.shape[0] // local_groups
    span = 1 << levels
    p = lax.broadcasted_iota(jnp.int32, (block, 1), 0)
    home = reversed_bits(p, levels) * (block // span) + p // span
    takes = []
    spots = arrived.shape[1]
    for g in range(2 * local_groups):
        index = home
        for bit in range(levels):
            count = block >> (bit + 1)
            moved = block + half * bit + (p % (1 << bit)) * count + home - reversed_bits(p, bit + 1) * count
            index = jnp.where((bit_of(p, bit) != bit_of(seq, bit)) & (dil[g] > (1 << bit)), moved, index)
        takes.append((index == lax.broadcasted_iota(jnp.int32, (block, spots), 1)).astype(BF))
    for copy in copies:
        copy.wait()
    total = jnp.zeros((block, out.shape[1]), F32) + bias[...]
    for c in range(2):
        for g in range(local_groups):
            offset = g * group_cols // 128 * 128
            wide = -(-(g * group_cols + group_cols - offset) // 128) * 128
            lane = lax.broadcasted_iota(jnp.int32, (1, wide), 1) + offset
            inside = (lane >= g * group_cols) & (lane < (g + 1) * group_cols)
            got = exact_dot(takes[c * local_groups + g], arrived[c, :, offset : offset + wide])
            mine = jnp.where(inside, got, 0.0).astype(BF)
            total = total + exact_dot(mine, weights[c, offset : offset + wide, :])
    out[...] = total.astype(BF)


def on_device(
    tiles, producer, slide_lengths, dilation, in_weight, in_bias, norm_gain, norm_bias,
    qkv_weight, qkv_bias, out_weight, out_bias,
):
    seq_n, tile_n = lax.axis_size("seq"), lax.axis_size("tile")
    devices = seq_n * tile_n
    me = lax.axis_index("seq") * tile_n + lax.axis_index("tile")
    capacity, width = tiles.shape[0], in_weight.shape[1]
    block = producer.shape[0] // devices
    per_pair = capacity // devices
    levels = min(16, seq_n).bit_length() - 1
    spots = block + (block // 2) * levels
    moves = (1 << levels) - 1
    vm = pl.BlockSpec(memory_space=pltpu.VMEM)
    sm = pl.BlockSpec(memory_space=pltpu.SMEM)
    dma = pltpu.SemaphoreType.DMA

    counts = jnp.sum((producer.reshape(devices, block) == me).astype(jnp.int32), axis=1)
    ids = jnp.arange(devices)
    starts = jnp.sum(jnp.where(ids[None, :] < ids[:, None], counts[None, :], 0), axis=1)
    slot = jnp.arange(per_pair, dtype=jnp.int32)
    pick = jnp.where(slot[None, :] < counts[:, None], starts[:, None] + slot[None, :], -1).reshape(-1, 1)
    own = lax.dynamic_slice_in_dim(producer, me * block, block, 0)

    placed, rows = pl.pallas_call(
        functools.partial(hand_over, levels),
        out_shape=(
            jax.ShapeDtypeStruct((block, width), BF),
            jax.ShapeDtypeStruct((tile_n, spots, width), BF),
        ),
        in_specs=[vm] * 7,
        out_specs=(vm, vm),
        scratch_shapes=[
            pltpu.VMEM((devices, per_pair, width), BF),
            pltpu.VMEM((devices, per_pair, width), BF),
            dma((devices - 1,)), dma((devices - 1,)), dma((moves,)), dma((moves,)),
            dma((moves + 1,)), dma((moves + 1,)),
        ],
        compiler_params=pltpu.CompilerParams(
            collective_id=0, has_side_effects=True, vmem_limit_bytes=VMEM_CAP
        ),
    )(
        tiles, in_weight, in_bias.reshape(1, -1), pick, own, norm_gain.reshape(1, -1), norm_bias.reshape(1, -1)
    )

    local_groups = dilation.shape[0] // tile_n
    local_cols = qkv_weight.shape[2]
    wide = -(-(local_cols // local_groups) // 128) * 128
    own_dil = lax.dynamic_slice_in_dim(dilation, lax.axis_index("tile") * local_groups, local_groups)
    back = pl.pallas_call(
        functools.partial(attend, levels, slide_lengths.shape[0]),
        out_shape=jax.ShapeDtypeStruct((tile_n, spots, local_cols), BF),
        in_specs=[sm, sm, vm, vm, vm],
        out_specs=vm,
        scratch_shapes=[
            pltpu.VMEM((2 * block, width), BF),
            pltpu.VMEM((2 * block, 1), jnp.int32),
            pltpu.VMEM((1, 2 * block), jnp.int32),
            pltpu.VMEM((2 * block, wide), BF),
        ],
        compiler_params=pltpu.CompilerParams(vmem_limit_bytes=VMEM_CAP),
    )(own_dil, jnp.cumsum(slide_lengths), rows, qkv_weight, qkv_bias)

    branch = pl.pallas_call(
        functools.partial(give_back, levels, local_groups),
        out_shape=jax.ShapeDtypeStruct((block, width), BF),
        in_specs=[sm, vm, vm, vm],
        out_specs=vm,
        scratch_shapes=[
            pltpu.VMEM((tile_n, spots, local_cols), BF),
            pltpu.VMEM((tile_n,) + out_weight.shape, BF),
            dma((2 * moves,)), dma((2 * moves,)), dma((2,)), dma((2,)),
        ],
        compiler_params=pltpu.CompilerParams(
            collective_id=1, has_side_effects=True, vmem_limit_bytes=VMEM_CAP
        ),
    )(dilation, back, out_weight, out_bias.reshape(1, -1))
    return (placed, branch)


def solution(mesh):
    return jax.shard_map(
        on_device,
        mesh=mesh,
        in_specs=(
            P(("grp", "seq", "tile"), None),
            P("grp", None),
            P("grp"),
            P(),
            P(),
            P(),
            P(),
            P(),
            P(None, None, "tile"),
            P(None, "tile"),
            P("tile", None),
            P(),
        ),
        out_specs=(P(("grp", "seq", "tile"), None), P(("grp", "seq", "tile"), None)),
        check_vma=False,
    )
```

```python
import functools
import math

import jax
import jax.numpy as jnp
from jax import lax
from jax.experimental import pallas as pl
from jax.experimental.pallas import tpu as pltpu
from jax.sharding import PartitionSpec as P

HEADS = 16
MESH = pl.DeviceIdType.MESH
BF = jnp.bfloat16
F32 = jnp.float32
VMEM_CAP = 56 * 1024 * 1024


def bit_of(value, bit):
    return (value // (1 << bit)) % 2


def reversed_bits(value, bits):
    total = 0
    for bit in range(bits):
        total = total + bit_of(value, bit) * (1 << (bits - 1 - bit))
    return total


def partner(seq, bit, low):
    span = 1 << bit
    return (seq // (2 * span)) * (2 * span) + (1 - bit_of(seq, bit)) * span + low


def exact_dot(a, b):
    return jnp.dot(a, b, preferred_element_type=F32)


def exchange_plan(levels):
    return [(bit, turn) for bit in reversed(range(levels)) for turn in range(1 << bit)]


def hand_over(
    levels, tiles, weight, bias, owners, gain, shift, placed, rows, outbox, inbox,
    send_a, recv_a, send_b, recv_b, send_c, recv_c,
):
    seq_n, tile_n = lax.axis_size("seq"), lax.axis_size("tile")
    devices = seq_n * tile_n
    seq, core = lax.axis_index("seq"), lax.axis_index("tile")
    other = 1 - core
    me = seq * tile_n + core
    per_pair = outbox.shape[1]
    block = owners.shape[2]
    width = outbox.shape[2]
    barrier = pltpu.get_barrier_semaphore()
    for k in range(1, devices):
        peer = (me + k) % devices
        pl.semaphore_signal(
            barrier, inc=1, device_id={"seq": peer // tile_n, "tile": peer % tile_n}, device_id_type=MESH
        )
    source = (exact_dot(tiles[...], weight[...]) + bias[...][None, :]).astype(BF)
    slots = devices * per_pair
    counts = jnp.sum((owners[...] == me).astype(jnp.int32), axis=2, keepdims=True)
    begin, begins = jnp.zeros((1, 1, 1), jnp.int32), []
    for at in range(devices):
        begins.append(begin)
        begin = begin + counts[at : at + 1]
    begins = jnp.concatenate(begins, axis=0)
    cube = (devices, per_pair, tiles.shape[0])
    nth = lax.broadcasted_iota(jnp.int32, cube, 2) - begins
    place = lax.broadcasted_iota(jnp.int32, cube, 1)
    chosen = jnp.where((nth == place) & (place < counts), 1.0, 0.0).reshape(slots, cube[2]).astype(BF)
    outbox[...] = exact_dot(chosen, source).reshape(devices, per_pair, width).astype(BF)
    pl.semaphore_wait(barrier, devices - 1)

    order = sorted(range(1, devices), key=lambda k: abs(k - devices // 2))
    first = []
    for k in order:
        peer = (me + k) % devices
        copy = pltpu.make_async_remote_copy(
            src_ref=outbox.at[peer], dst_ref=inbox.at[me], send_sem=send_a.at[k - 1], recv_sem=recv_a.at[k - 1],
            device_id={"seq": peer // tile_n, "tile": peer % tile_n}, device_id_type=MESH,
        )
        copy.start()
        first.append(copy)
    inbox[me] = outbox[me]
    own = owners[me]
    onehot = (own == lax.broadcasted_iota(jnp.int32, (128, block), 0)).astype(F32)
    row_i = lax.broadcasted_iota(jnp.int32, (block, block), 0)
    col_i = lax.broadcasted_iota(jnp.int32, (block, block), 1)
    before = exact_dot(onehot.astype(BF), (row_i < col_i).astype(BF))
    rank = jnp.sum(before * onehot, axis=0, keepdims=True).astype(jnp.int32)
    slot = own * per_pair + rank
    landing = (slot == lax.broadcasted_iota(jnp.int32, (slots, block), 0)).astype(F32).T.astype(BF)
    span = 1 << levels
    stretch = block // span
    reorder = (reversed_bits(row_i // stretch, levels) + span * (row_i % stretch) == col_i).astype(BF)
    for copy in first:
        copy.wait_recv()
    got = inbox[...].astype(F32).reshape(slots, width).astype(BF)
    embedded = exact_dot(landing, got)
    placed[...] = embedded.astype(BF)
    center = embedded - jnp.mean(embedded, axis=1, keepdims=True)
    spread = jnp.mean(center * center, axis=1, keepdims=True)
    normed = (center * lax.rsqrt(spread + 1e-05) * gain[...][None, :] + shift[...][None, :]).astype(BF)
    rows[core, 0:block] = exact_dot(reorder, normed).astype(BF)

    second, forwards = [], []
    half = block // 2
    for at, (bit, turn) in enumerate(exchange_plan(levels)):
        count = block >> (bit + 1)
        to = partner(seq, bit, (seq + turn) % (1 << bit))
        start = pl.multiple_of(reversed_bits(to, bit + 1) * count, count)
        land = pl.multiple_of(block + half * bit + (seq % (1 << bit)) * count, count)
        copy = pltpu.make_async_remote_copy(
            src_ref=rows.at[core, pl.ds(start, count)], dst_ref=rows.at[core, pl.ds(land, count)],
            send_sem=send_b.at[at], recv_sem=recv_b.at[at],
            device_id={"seq": to, "tile": core}, device_id_type=MESH,
        )
        copy.start()
        second.append(copy)
    last = len(second)
    copy = pltpu.make_async_remote_copy(
        src_ref=rows.at[core, pl.ds(0, block)], dst_ref=rows.at[core, pl.ds(0, block)],
        send_sem=send_c.at[last], recv_sem=recv_c.at[last],
        device_id={"seq": seq, "tile": other}, device_id_type=MESH,
    )
    copy.start()
    forwards.append(copy)
    for at, (bit, turn) in reversed(list(enumerate(exchange_plan(levels)))):
        count = block >> (bit + 1)
        low = (seq % (1 << bit) + (1 << bit) - turn) % (1 << bit)
        land = pl.multiple_of(block + half * bit + low * count, count)
        second[at].wait_recv()
        copy = pltpu.make_async_remote_copy(
            src_ref=rows.at[core, pl.ds(land, count)], dst_ref=rows.at[core, pl.ds(land, count)],
            send_sem=send_c.at[at], recv_sem=recv_c.at[at],
            device_id={"seq": seq, "tile": other}, device_id_type=MESH,
        )
        copy.start()
        forwards.append(copy)
    for copy in first + second:
        copy.wait_send()
    for copy in forwards:
        copy.wait()


def chunk_list(seq, level, block):
    width = block >> level
    sub = reversed_bits(seq, level) * width
    found = [(sub, seq % (1 << level))]
    for bit in range(level):
        count = block >> (bit + 1)
        inner = sub - reversed_bits(seq, bit + 1) * count
        for low in range(1 << bit):
            found.append(
                (block + (block // 2) * bit + low * count + inner, partner(seq, bit, low) % (1 << level))
            )
    return [(pl.multiple_of(a, width), pl.multiple_of(c * width, width)) for a, c in found]


def attend(
    levels, slides, dilation, lengths, rows, weight, bias, embedded, back, kept, picked, id_col, id_row, mixed, sem
):
    keep = pltpu.make_async_copy(embedded, kept, sem)
    keep.start()
    seq = lax.axis_index("seq")
    ends = [lengths[0]]
    for at in range(1, slides):
        ends.append(ends[-1] + lengths[at])
    groups = dilation.shape[0] // lax.axis_size("tile")
    dil = [dilation[lax.axis_index("tile") * groups + g] for g in range(groups)]
    block = picked.shape[0] // 2
    total = 2 * block
    group_cols = weight.shape[2] // groups
    head_dim = weight.shape[1] // HEADS
    heads_here = group_cols // head_dim
    factor = math.log2(math.e) / math.sqrt(head_dim)
    span = 1 << levels
    stretch = block // span
    back[...] = jnp.zeros_like(back)

    def slide_of(n, level):
        size = block >> level
        v = n % size
        pos = (
            ((seq >> level) << level) * total + ((n % block) // size) * total + (n // block) * block
            + seq % (1 << level)
            + (reversed_bits(v // stretch, levels - level) << level)
            + span * (v % stretch)
        )
        out = jnp.zeros_like(n)
        for at in range(slides):
            out = out + (pos >= ends[at]).astype(jnp.int32)
        return out

    for g in range(groups):
        offset = g * group_cols // 128 * 128
        wide = -(-(g * group_cols + group_cols - offset) // 128) * 128
        for level in range(levels + 1):
            @pl.when(dil[g] == 1 << level)
            def _():
                size = block >> level
                for side in range(2):
                    for start, put in chunk_list(seq, level, block):
                        picked[pl.ds(side * block + put, size), :] = rows[side, pl.ds(start, size), :]
                id_col[...] = slide_of(lax.broadcasted_iota(jnp.int32, (total, 1), 0), level)
                id_row[...] = slide_of(lax.broadcasted_iota(jnp.int32, (1, total), 1), level)

        x = picked[...]
        triple = [
            (exact_dot(x, weight[m, :, offset : offset + wide]) + bias[m : m + 1, offset : offset + wide]).astype(BF)
            for m in range(3)
        ]
        queries, keys, values = triple
        closed = jnp.where(id_col[...] == id_row[...], 0.0, -1e30)
        lane = lax.broadcasted_iota(jnp.int32, (1, wide), 1)
        result = jnp.zeros((total, wide), F32)
        for h in range(heads_here):
            low = g * group_cols - offset + h * head_dim
            inside = (lane >= low) & (lane < low + head_dim)
            scores = lax.dot_general(
                jnp.where(inside, queries, jnp.zeros((), BF)), keys, (((1,), (1,)), ((), ())),
                preferred_element_type=F32,
            ) + closed
            peak = jnp.max(scores, axis=1, keepdims=True)
            weights = jnp.exp2((scores - peak) * factor)
            norm = jnp.sum(weights, axis=1, keepdims=True)
            result = jnp.where(inside, exact_dot(weights.astype(BF), values) / norm, result)
        mixed[...] = result.astype(BF)
        for level in range(levels + 1):
            @pl.when(dil[g] == 1 << level)
            def _():
                size = block >> level
                for side in range(2):
                    for start, put in chunk_list(seq, level, block):
                        back[side, pl.ds(start, size), offset : offset + wide] += mixed[
                            pl.ds(side * block + put, size), :
                        ]
    keep.wait()


def give_back(
    levels, local_groups, dil, back, weight, bias, out, arrived, weights, send_a, recv_a, send_b, recv_b
):
    seq, core = lax.axis_index("seq"), lax.axis_index("tile")
    other = 1 - core
    block = out.shape[0]
    half = block // 2
    plan = exchange_plan(levels)
    barrier = pltpu.get_barrier_semaphore()
    peers = []
    for bit, turn in plan:
        to = partner(seq, bit, (seq + turn) % (1 << bit))
        peers += [{"seq": to, "tile": core}, {"seq": to, "tile": other}]
    sibling = {"seq": seq, "tile": other}
    for device in peers + [sibling]:
        pl.semaphore_signal(barrier, inc=1, device_id=device, device_id_type=MESH)
    pl.semaphore_wait(barrier, len(peers) + 1)
    copies = []
    for at, (bit, turn) in enumerate(plan):
        count = block >> (bit + 1)
        low = (seq + turn) % (1 << bit)
        start = pl.multiple_of(block + half * bit + low * count, count)
        land = pl.multiple_of(block + half * bit + (seq % (1 << bit)) * count, count)
        for rel in range(2):
            side = (core + rel) % 2
            copy = pltpu.make_async_remote_copy(
                src_ref=back.at[side, pl.ds(start, count)], dst_ref=arrived.at[core, pl.ds(land, count)],
                send_sem=send_a.at[2 * at + rel], recv_sem=recv_a.at[2 * at + rel],
                device_id={"seq": partner(seq, bit, low), "tile": side}, device_id_type=MESH,
            )
            copy.start()
            copies.append(copy)
    for at, (src, dst) in enumerate(
        [(back.at[other, pl.ds(0, block)], arrived.at[core, pl.ds(0, block)]), (weight, weights.at[core])]
    ):
        copy = pltpu.make_async_remote_copy(
            src_ref=src, dst_ref=dst, send_sem=send_b.at[at], recv_sem=recv_b.at[at],
            device_id=sibling, device_id_type=MESH,
        )
        copy.start()
        copies.append(copy)
    arrived[core, 0:block] = back[core, 0:block]
    weights[core] = weight[...]
    group_cols = weight.shape[0] // local_groups
    span = 1 << levels
    p = lax.broadcasted_iota(jnp.int32, (block, 1), 0)
    home = reversed_bits(p, levels) * (block // span) + p // span
    takes = []
    spots = arrived.shape[1]
    for g in range(2 * local_groups):
        index = home
        for bit in range(levels):
            count = block >> (bit + 1)
            moved = block + half * bit + (p % (1 << bit)) * count + home - reversed_bits(p, bit + 1) * count
            index = jnp.where((bit_of(p, bit) != bit_of(seq, bit)) & (dil[g] > (1 << bit)), moved, index)
        takes.append((index == lax.broadcasted_iota(jnp.int32, (block, spots), 1)).astype(BF))
    for copy in copies:
        copy.wait()
    total = jnp.zeros((block, out.shape[1]), F32) + bias[...][None, :]
    for c in range(2):
        for g in range(local_groups):
            offset = g * group_cols // 128 * 128
            wide = -(-(g * group_cols + group_cols - offset) // 128) * 128
            lane = lax.broadcasted_iota(jnp.int32, (1, wide), 1) + offset
            inside = (lane >= g * group_cols) & (lane < (g + 1) * group_cols)
            got = exact_dot(takes[c * local_groups + g], arrived[c, :, offset : offset + wide])
            mine = jnp.where(inside, got, 0.0).astype(BF)
            total = total + exact_dot(mine, weights[c, offset : offset + wide, :])
    out[...] = total.astype(BF)


def on_device(
    tiles, producer, slide_lengths, dilation, in_weight, in_bias, norm_gain, norm_bias,
    qkv_weight, qkv_bias, out_weight, out_bias,
):
    seq_n, tile_n = lax.axis_size("seq"), lax.axis_size("tile")
    devices = seq_n * tile_n
    capacity, width = tiles.shape[0], in_weight.shape[1]
    block = producer.shape[0] // devices
    per_pair = capacity // devices
    levels = min(16, seq_n).bit_length() - 1
    spots = block + (block // 2) * levels
    moves = (1 << levels) - 1
    vm = pl.BlockSpec(memory_space=pltpu.VMEM)
    hbm = pl.BlockSpec(memory_space=pl.ANY)
    sm = pl.BlockSpec(memory_space=pltpu.SMEM)
    dma = pltpu.SemaphoreType.DMA

    placed, rows = pl.pallas_call(
        functools.partial(hand_over, levels),
        out_shape=(
            jax.ShapeDtypeStruct((block, width), BF),
            jax.ShapeDtypeStruct((tile_n, spots, width), BF),
        ),
        in_specs=[vm] * 6,
        out_specs=(vm, vm),
        scratch_shapes=[
            pltpu.VMEM((devices, per_pair, width), BF),
            pltpu.VMEM((devices, per_pair, width), BF),
            dma((devices - 1,)), dma((devices - 1,)), dma((moves,)), dma((moves,)),
            dma((moves + 1,)), dma((moves + 1,)),
        ],
        compiler_params=pltpu.CompilerParams(
            collective_id=0, has_side_effects=True, vmem_limit_bytes=VMEM_CAP
        ),
    )(
        tiles, in_weight, in_bias, producer.reshape(devices, 1, block), norm_gain, norm_bias
    )

    local_groups = dilation.shape[0] // tile_n
    local_cols = qkv_weight.shape[2]
    wide = -(-(local_cols // local_groups) // 128) * 128
    back, kept = pl.pallas_call(
        functools.partial(attend, levels, slide_lengths.shape[0]),
        out_shape=(
            jax.ShapeDtypeStruct((tile_n, spots, local_cols), BF),
            jax.ShapeDtypeStruct((block, width), BF),
        ),
        in_specs=[sm, sm, vm, vm, vm, hbm],
        out_specs=(vm, hbm),
        scratch_shapes=[
            pltpu.VMEM((2 * block, width), BF),
            pltpu.VMEM((2 * block, 1), jnp.int32),
            pltpu.VMEM((1, 2 * block), jnp.int32),
            pltpu.VMEM((2 * block, wide), BF),
            dma,
        ],
        compiler_params=pltpu.CompilerParams(vmem_limit_bytes=VMEM_CAP),
    )(dilation, slide_lengths, rows, qkv_weight, qkv_bias, placed)

    branch = pl.pallas_call(
        functools.partial(give_back, levels, local_groups),
        out_shape=jax.ShapeDtypeStruct((block, width), BF),
        in_specs=[sm, vm, vm, vm],
        out_specs=vm,
        scratch_shapes=[
            pltpu.VMEM((tile_n, spots, local_cols), BF),
            pltpu.VMEM((tile_n,) + out_weight.shape, BF),
            dma((2 * moves,)), dma((2 * moves,)), dma((2,)), dma((2,)),
        ],
        compiler_params=pltpu.CompilerParams(
            collective_id=1, has_side_effects=True, vmem_limit_bytes=VMEM_CAP
        ),
    )(dilation, back, out_weight, out_bias)
    return (kept, branch)


def solution(mesh):
    return jax.shard_map(
        on_device,
        mesh=mesh,
        in_specs=(
            P(("grp", "seq", "tile"), None),
            P("grp", None),
            P("grp"),
            P(),
            P(),
            P(),
            P(),
            P(),
            P(None, None, "tile"),
            P(None, "tile"),
            P("tile", None),
            P(),
        ),
        out_specs=(P(("grp", "seq", "tile"), None), P(("grp", "seq", "tile"), None)),
        check_vma=False,
    )
```

```python
import functools
import math

import jax
import jax.numpy as jnp
from jax import lax
from jax.experimental import pallas as pl
from jax.experimental.pallas import tpu as pltpu
from jax.sharding import PartitionSpec as P

HEADS = 16
MESH = pl.DeviceIdType.MESH
BF = jnp.bfloat16
F32 = jnp.float32
VMEM_CAP = 56 * 1024 * 1024


def bit_of(value, bit):
    return (value // (1 << bit)) % 2


def reversed_bits(value, bits):
    total = 0
    for bit in range(bits):
        total = total + bit_of(value, bit) * (1 << (bits - 1 - bit))
    return total


def partner(seq, bit, low):
    span = 1 << bit
    return (seq // (2 * span)) * (2 * span) + (1 - bit_of(seq, bit)) * span + low


def exact_dot(a, b):
    return jnp.dot(a, b, preferred_element_type=F32)


def exchange_plan(levels):
    return [(bit, turn) for bit in reversed(range(levels)) for turn in range(1 << bit)]


def hand_over(
    levels, tiles, weight, bias, owners, gain, shift, placed, rows, outbox, inbox,
    send_a, recv_a, send_b, recv_b, send_c, recv_c,
):
    seq_n, tile_n = lax.axis_size("seq"), lax.axis_size("tile")
    devices = seq_n * tile_n
    seq, core = lax.axis_index("seq"), lax.axis_index("tile")
    other = 1 - core
    me = seq * tile_n + core
    per_pair = outbox.shape[1]
    block = owners.shape[2]
    width = outbox.shape[2]
    barrier = pltpu.get_barrier_semaphore()
    for k in range(1, devices):
        peer = (me + k) % devices
        pl.semaphore_signal(
            barrier, inc=1, device_id={"seq": peer // tile_n, "tile": peer % tile_n}, device_id_type=MESH
        )
    source = (exact_dot(tiles[...], weight[...]) + bias[...][None, :]).astype(BF)
    slots = devices * per_pair
    counts = jnp.sum((owners[...] == me).astype(jnp.int32), axis=2, keepdims=True)
    begin, begins = jnp.zeros((1, 1, 1), jnp.int32), []
    for at in range(devices):
        begins.append(begin)
        begin = begin + counts[at : at + 1]
    begins = jnp.concatenate(begins, axis=0)
    cube = (devices, per_pair, tiles.shape[0])
    nth = lax.broadcasted_iota(jnp.int32, cube, 2) - begins
    place = lax.broadcasted_iota(jnp.int32, cube, 1)
    chosen = jnp.where((nth == place) & (place < counts), 1.0, 0.0).reshape(slots, cube[2]).astype(BF)
    outbox[...] = exact_dot(chosen, source).reshape(devices, per_pair, width).astype(BF)
    pl.semaphore_wait(barrier, devices - 1)

    order = sorted(range(1, devices), key=lambda k: abs(k - devices // 2))
    first = []
    for k in order:
        peer = (me + k) % devices
        copy = pltpu.make_async_remote_copy(
            src_ref=outbox.at[peer], dst_ref=inbox.at[me], send_sem=send_a.at[k - 1], recv_sem=recv_a.at[k - 1],
            device_id={"seq": peer // tile_n, "tile": peer % tile_n}, device_id_type=MESH,
        )
        copy.start()
        first.append(copy)
    inbox[me] = outbox[me]
    own = owners[me]
    onehot = (own == lax.broadcasted_iota(jnp.int32, (128, block), 0)).astype(F32)
    row_i = lax.broadcasted_iota(jnp.int32, (block, block), 0)
    col_i = lax.broadcasted_iota(jnp.int32, (block, block), 1)
    before = exact_dot(onehot.astype(BF), (row_i < col_i).astype(BF))
    rank = jnp.sum(before * onehot, axis=0, keepdims=True).astype(jnp.int32)
    slot = own * per_pair + rank
    landing = (slot == lax.broadcasted_iota(jnp.int32, (slots, block), 0)).astype(F32).T.astype(BF)
    span = 1 << levels
    stretch = block // span
    reorder = (reversed_bits(row_i // stretch, levels) + span * (row_i % stretch) == col_i).astype(BF)
    for copy in first:
        copy.wait_recv()
    got = inbox[...].astype(F32).reshape(slots, width).astype(BF)
    embedded = exact_dot(landing, got)
    placed[...] = embedded.astype(BF)
    center = embedded - jnp.mean(embedded, axis=1, keepdims=True)
    spread = jnp.mean(center * center, axis=1, keepdims=True)
    normed = (center * lax.rsqrt(spread + 1e-05) * gain[...][None, :] + shift[...][None, :]).astype(BF)
    rows[core, 0:block] = exact_dot(reorder, normed).astype(BF)

    second, forwards = [], []
    half = block // 2
    for at, (bit, turn) in enumerate(exchange_plan(levels)):
        count = block >> (bit + 1)
        to = partner(seq, bit, (seq + turn) % (1 << bit))
        start = pl.multiple_of(reversed_bits(to, bit + 1) * count, count)
        land = pl.multiple_of(block + half * bit + (seq % (1 << bit)) * count, count)
        copy = pltpu.make_async_remote_copy(
            src_ref=rows.at[core, pl.ds(start, count)], dst_ref=rows.at[core, pl.ds(land, count)],
            send_sem=send_b.at[at], recv_sem=recv_b.at[at],
            device_id={"seq": to, "tile": core}, device_id_type=MESH,
        )
        copy.start()
        second.append(copy)
    last = len(second)
    copy = pltpu.make_async_remote_copy(
        src_ref=rows.at[core, pl.ds(0, block)], dst_ref=rows.at[core, pl.ds(0, block)],
        send_sem=send_c.at[last], recv_sem=recv_c.at[last],
        device_id={"seq": seq, "tile": other}, device_id_type=MESH,
    )
    copy.start()
    forwards.append(copy)
    for at, (bit, turn) in reversed(list(enumerate(exchange_plan(levels)))):
        count = block >> (bit + 1)
        low = (seq % (1 << bit) + (1 << bit) - turn) % (1 << bit)
        land = pl.multiple_of(block + half * bit + low * count, count)
        second[at].wait_recv()
        copy = pltpu.make_async_remote_copy(
            src_ref=rows.at[core, pl.ds(land, count)], dst_ref=rows.at[core, pl.ds(land, count)],
            send_sem=send_c.at[at], recv_sem=recv_c.at[at],
            device_id={"seq": seq, "tile": other}, device_id_type=MESH,
        )
        copy.start()
        forwards.append(copy)
    for copy in first + second:
        copy.wait_send()
    for copy in forwards:
        copy.wait()


def chunk_list(seq, level, block):
    width = block >> level
    sub = reversed_bits(seq, level) * width
    found = [(sub, seq % (1 << level))]
    for bit in range(level):
        count = block >> (bit + 1)
        inner = sub - reversed_bits(seq, bit + 1) * count
        for low in range(1 << bit):
            found.append(
                (block + (block // 2) * bit + low * count + inner, partner(seq, bit, low) % (1 << level))
            )
    return [(pl.multiple_of(a, width), pl.multiple_of(c * width, width)) for a, c in found]


def attend(
    levels, slides, dilation, lengths, rows, weight, bias, embedded, back, kept, picked, id_col, id_row, mixed, sem
):
    keep = pltpu.make_async_copy(embedded, kept, sem)
    keep.start()
    seq = lax.axis_index("seq")
    ends = [lengths[0]]
    for at in range(1, slides):
        ends.append(ends[-1] + lengths[at])
    groups = dilation.shape[0] // lax.axis_size("tile")
    dil = [dilation[lax.axis_index("tile") * groups + g] for g in range(groups)]
    block = picked.shape[0] // 2
    total = 2 * block
    group_cols = weight.shape[2] // groups
    head_dim = weight.shape[1] // HEADS
    heads_here = group_cols // head_dim
    factor = math.log2(math.e) / math.sqrt(head_dim)
    span = 1 << levels
    stretch = block // span
    back[...] = jnp.zeros_like(back)

    def slide_of(n, level):
        size = block >> level
        v = n % size
        pos = (
            ((seq >> level) << level) * total + ((n % block) // size) * total + (n // block) * block
            + seq % (1 << level)
            + (reversed_bits(v // stretch, levels - level) << level)
            + span * (v % stretch)
        )
        out = jnp.zeros_like(n)
        for at in range(slides):
            out = out + (pos >= ends[at]).astype(jnp.int32)
        return out

    for g in range(groups):
        offset = g * group_cols // 128 * 128
        wide = -(-(g * group_cols + group_cols - offset) // 128) * 128
        for level in range(levels + 1):
            @pl.when(dil[g] == 1 << level)
            def _():
                size = block >> level
                for side in range(2):
                    for start, put in chunk_list(seq, level, block):
                        picked[pl.ds(side * block + put, size), :] = rows[side, pl.ds(start, size), :]
                id_col[...] = slide_of(lax.broadcasted_iota(jnp.int32, (total, 1), 0), level)
                id_row[...] = slide_of(lax.broadcasted_iota(jnp.int32, (1, total), 1), level)

        x = picked[...]
        triple = [
            (exact_dot(x, weight[m, :, offset : offset + wide]) + bias[m : m + 1, offset : offset + wide]).astype(BF)
            for m in range(3)
        ]
        queries, keys, values = triple
        closed = jnp.where(id_col[...] == id_row[...], 0.0, -1e30)
        lane = lax.broadcasted_iota(jnp.int32, (1, wide), 1)
        result = jnp.zeros((total, wide), F32)
        for h in range(heads_here):
            low = g * group_cols - offset + h * head_dim
            inside = (lane >= low) & (lane < low + head_dim)
            scores = lax.dot_general(
                jnp.where(inside, queries, jnp.zeros((), BF)), keys, (((1,), (1,)), ((), ())),
                preferred_element_type=F32,
            ) + closed
            peak = jnp.max(scores, axis=1, keepdims=True)
            weights = jnp.exp2((scores - peak) * factor)
            norm = jnp.sum(weights, axis=1, keepdims=True)
            result = jnp.where(inside, exact_dot(weights.astype(BF), values) / norm, result)
        mixed[...] = result.astype(BF)
        for level in range(levels + 1):
            @pl.when(dil[g] == 1 << level)
            def _():
                size = block >> level
                for side in range(2):
                    for start, put in chunk_list(seq, level, block):
                        back[side, pl.ds(start, size), offset : offset + wide] += mixed[
                            pl.ds(side * block + put, size), :
                        ]
    keep.wait()


def give_back(
    levels, local_groups, dil, back, weight, bias, out, arrived, weights, send_a, recv_a, send_b, recv_b
):
    seq, core = lax.axis_index("seq"), lax.axis_index("tile")
    other = 1 - core
    block = out.shape[0]
    half = block // 2
    plan = exchange_plan(levels)
    barrier = pltpu.get_barrier_semaphore()
    peers = []
    for bit, turn in plan:
        to = partner(seq, bit, (seq + turn) % (1 << bit))
        peers += [{"seq": to, "tile": core}, {"seq": to, "tile": other}]
    sibling = {"seq": seq, "tile": other}
    for device in peers + [sibling]:
        pl.semaphore_signal(barrier, inc=1, device_id=device, device_id_type=MESH)
    pl.semaphore_wait(barrier, len(peers) + 1)
    copies = []
    for at, (bit, turn) in enumerate(plan):
        count = block >> (bit + 1)
        low = (seq + turn) % (1 << bit)
        start = pl.multiple_of(block + half * bit + low * count, count)
        land = pl.multiple_of(block + half * bit + (seq % (1 << bit)) * count, count)
        for rel in range(2):
            side = (core + rel) % 2
            copy = pltpu.make_async_remote_copy(
                src_ref=back.at[side, pl.ds(start, count)], dst_ref=arrived.at[core, pl.ds(land, count)],
                send_sem=send_a.at[2 * at + rel], recv_sem=recv_a.at[2 * at + rel],
                device_id={"seq": partner(seq, bit, low), "tile": side}, device_id_type=MESH,
            )
            copy.start()
            copies.append(copy)
    for at, (src, dst) in enumerate(
        [(back.at[other, pl.ds(0, block)], arrived.at[core, pl.ds(0, block)]), (weight, weights.at[core])]
    ):
        copy = pltpu.make_async_remote_copy(
            src_ref=src, dst_ref=dst, send_sem=send_b.at[at], recv_sem=recv_b.at[at],
            device_id=sibling, device_id_type=MESH,
        )
        copy.start()
        copies.append(copy)
    arrived[core, 0:block] = back[core, 0:block]
    weights[core] = weight[...]
    group_cols = weight.shape[0] // local_groups
    span = 1 << levels
    p = lax.broadcasted_iota(jnp.int32, (block, 1), 0)
    home = reversed_bits(p, levels) * (block // span) + p // span
    takes = []
    spots = arrived.shape[1]
    for g in range(2 * local_groups):
        index = home
        for bit in range(levels):
            count = block >> (bit + 1)
            moved = block + half * bit + (p % (1 << bit)) * count + home - reversed_bits(p, bit + 1) * count
            index = jnp.where((bit_of(p, bit) != bit_of(seq, bit)) & (dil[g] > (1 << bit)), moved, index)
        takes.append((index == lax.broadcasted_iota(jnp.int32, (block, spots), 1)).astype(BF))
    for copy in copies:
        copy.wait()
    total = jnp.zeros((block, out.shape[1]), F32) + bias[...][None, :]
    for c in range(2):
        for g in range(local_groups):
            offset = g * group_cols // 128 * 128
            wide = -(-(g * group_cols + group_cols - offset) // 128) * 128
            lane = lax.broadcasted_iota(jnp.int32, (1, wide), 1) + offset
            inside = (lane >= g * group_cols) & (lane < (g + 1) * group_cols)
            got = exact_dot(takes[c * local_groups + g], arrived[c, :, offset : offset + wide])
            mine = jnp.where(inside, got, 0.0).astype(BF)
            total = total + exact_dot(mine, weights[c, offset : offset + wide, :])
    out[...] = total.astype(BF)


def on_device(
    tiles, producer, slide_lengths, dilation, in_weight, in_bias, norm_gain, norm_bias,
    qkv_weight, qkv_bias, out_weight, out_bias,
):
    seq_n, tile_n = lax.axis_size("seq"), lax.axis_size("tile")
    devices = seq_n * tile_n
    capacity, width = tiles.shape[0], in_weight.shape[1]
    block = producer.shape[0] // devices
    per_pair = capacity // devices
    levels = min(16, seq_n).bit_length() - 1
    spots = block + (block // 2) * levels
    moves = (1 << levels) - 1
    vm = pl.BlockSpec(memory_space=pltpu.VMEM)
    hbm = pl.BlockSpec(memory_space=pl.ANY)
    sm = pl.BlockSpec(memory_space=pltpu.SMEM)
    dma = pltpu.SemaphoreType.DMA

    placed, rows = pl.pallas_call(
        functools.partial(hand_over, levels),
        out_shape=(
            jax.ShapeDtypeStruct((block, width), BF),
            jax.ShapeDtypeStruct((tile_n, spots, width), BF),
        ),
        in_specs=[vm] * 6,
        out_specs=(vm, vm),
        scratch_shapes=[
            pltpu.VMEM((devices, per_pair, width), BF),
            pltpu.VMEM((devices, per_pair, width), BF),
            dma((devices - 1,)), dma((devices - 1,)), dma((moves,)), dma((moves,)),
            dma((moves + 1,)), dma((moves + 1,)),
        ],
        compiler_params=pltpu.CompilerParams(
            collective_id=0, has_side_effects=True, vmem_limit_bytes=VMEM_CAP
        ),
    )(
        tiles, in_weight, in_bias, producer.reshape(devices, 1, block), norm_gain, norm_bias
    )

    local_groups = dilation.shape[0] // tile_n
    local_cols = qkv_weight.shape[2]
    wide = -(-(local_cols // local_groups) // 128) * 128
    back, kept = pl.pallas_call(
        functools.partial(attend, levels, slide_lengths.shape[0]),
        out_shape=(
            jax.ShapeDtypeStruct((tile_n, spots, local_cols), BF),
            jax.ShapeDtypeStruct((block, width), BF),
        ),
        in_specs=[sm, sm, vm, vm, vm, hbm],
        out_specs=(vm, vm),
        scratch_shapes=[
            pltpu.VMEM((2 * block, width), BF),
            pltpu.VMEM((2 * block, 1), jnp.int32),
            pltpu.VMEM((1, 2 * block), jnp.int32),
            pltpu.VMEM((2 * block, wide), BF),
            dma,
        ],
        compiler_params=pltpu.CompilerParams(vmem_limit_bytes=VMEM_CAP),
    )(dilation, slide_lengths, rows, qkv_weight, qkv_bias, placed)

    branch = pl.pallas_call(
        functools.partial(give_back, levels, local_groups),
        out_shape=jax.ShapeDtypeStruct((block, width), BF),
        in_specs=[sm, vm, vm, vm],
        out_specs=vm,
        scratch_shapes=[
            pltpu.VMEM((tile_n, spots, local_cols), BF),
            pltpu.VMEM((tile_n,) + out_weight.shape, BF),
            dma((2 * moves,)), dma((2 * moves,)), dma((2,)), dma((2,)),
        ],
        compiler_params=pltpu.CompilerParams(
            collective_id=1, has_side_effects=True, vmem_limit_bytes=VMEM_CAP
        ),
    )(dilation, back, out_weight, out_bias)
    return (kept, branch)


def solution(mesh):
    return jax.shard_map(
        on_device,
        mesh=mesh,
        in_specs=(
            P(("grp", "seq", "tile"), None),
            P("grp", None),
            P("grp"),
            P(),
            P(),
            P(),
            P(),
            P(),
            P(None, None, "tile"),
            P(None, "tile"),
            P("tile", None),
            P(),
        ),
        out_specs=(P(("grp", "seq", "tile"), None), P(("grp", "seq", "tile"), None)),
        check_vma=False,
    )
```
